512 devices in a mesh: grp: 16 (over z), feat: 32 (over y, x, core).
Axes of the slice: x: 4, y: 4, z: 16, core: 2. Of those that a mesh axis runs over, the one named last changes fastest.
Arguments:
- starting_latent_vectors: float32 [2048, 384], P(('grp', 'feat')), may hold values from -6 to 6
- run_driver_case: int32 [2048], P(('grp', 'feat')), may hold values from 0 to 7
- pair_table: int32 [2, 73920], P(None, 'feat'), may hold values from 0 to 383, as said below
- quadratic: bfloat16 [73920, 384], P('feat'), may hold values from -0.0234375 to 0.0234375
- linear: bfloat16 [384, 384], P('feat'), may hold values from -0.3125 to 0.3125
- forcing: float32 [8, 384], replicated, may hold values from -6 to 6
- basis: bfloat16 [2, 172032, 384], P(None, ('grp', 'feat')), may hold values from -0.3125 to 0.3125
- mean_fields: float32 [2, 172032], P(None, ('grp', 'feat')), may hold values from 1.5 to 3
Outputs:
- specific_weight_array: bfloat16 [172032, 2048], P(('grp', 'feat'))
- dimensionless_heat_measure: bfloat16 [172032, 2048], P(('grp', 'feat'))
The draws below stay inside these ranges and needn't reach their ends.
Inputs may be any that keep to these rules, and one draw needn't show every extreme that they name: `pair_table`: every pair i <= j of state indices appears in exactly one column, with i in row 0 and j in row 1; columns are in a drawn order.
All inputs are finite; a program needn't handle non-finite values.
Results may differ from the reference program's by a relative error of at most 0.0065.
Values may be sent and summed in bfloat16 or wider, within the bound.
A program may use at most 64 MiB of HBM per device.

```python
import math
import jax
import jax.numpy as jnp
import numpy as np
from jax import lax

LATENT_WIDTH = 384
PAIRS = 73920
STEPS = 2
DRIVER_CASES = 8
OUTLOOK_TRIALS = 2048
SPATIAL_POINTS = 172032


def draw_pair_table(key, part):
    first_list, second_list = np.triu_indices(LATENT_WIDTH)
    order = jax.random.permutation(jax.random.fold_in(key, 11), LATENT_WIDTH * (LATENT_WIDTH + 1) // 2)
    first_index = jnp.asarray(first_list.astype(np.int32))[order]
    second_index = jnp.asarray(second_list.astype(np.int32))[order]
    return jnp.stack([first_index, second_index]).astype(jnp.int32)


def place_ends(result, key, least, top_value):
    place = [jax.random.randint(jax.random.fold_in(key, axis), (), 0, length) for axis, length in enumerate(result.shape)]
    longest = result.shape.index(max(result.shape))
    neighbour = place[:longest] + [(place[longest] + 1) % result.shape[longest]] + place[longest + 1:]
    return result.at[tuple(place)].set(least).at[tuple(neighbour)].set(top_value)


def level_of(own_key, extent, cuts, low, top_value):
    def one(dim, shards_of):
        draws = jax.random.uniform(jax.random.fold_in(jax.random.fold_in(own_key, 6), dim), (shards_of,), jnp.float32, low / len(cuts), top_value / len(cuts))
        return jnp.repeat(jnp.exp(draws), extent[dim] // shards_of).reshape((-1,) + (1,) * (len(extent) - dim - 1))

    factor_of = one(*cuts[0])
    for cut in cuts[1:]:
        factor_of = factor_of * one(*cut)
    return factor_of


def normal_values(stream_key, shape, spread, most, cuts=(), held_as=jnp.bfloat16):
    loudness = level_of(stream_key, shape, cuts, -0.22, 0.18) if cuts else 1.0
    entries = jax.random.normal(stream_key, shape, jnp.float32) * spread * loudness
    return jnp.minimum(jnp.maximum(entries, -most), most).astype(held_as)


def setup_inputs(seed: int = 0) -> dict:
    key_of = jax.random.split(jax.random.key(seed), 9)
    starting_latent_vectors = normal_values(key_of[0], (OUTLOOK_TRIALS, LATENT_WIDTH), 1.0, 6.0, ((0, 512),), jnp.float32)
    run_driver_case = place_ends(jax.random.randint(key_of[1], (OUTLOOK_TRIALS,), 0, DRIVER_CASES), jax.random.fold_in(key_of[1], 1), 0, DRIVER_CASES - 1).astype(jnp.int32)
    pair_table = draw_pair_table(jax.random.fold_in(key_of[8], 71), 0)
    quadratic = normal_values(key_of[3], (PAIRS, LATENT_WIDTH), PAIRS ** -0.5, 0.0234375, ((0, 32),))
    linear = normal_values(key_of[4], (LATENT_WIDTH, LATENT_WIDTH), LATENT_WIDTH ** -0.5, 0.3125, ((0, 32),))
    forcing = normal_values(key_of[5], (DRIVER_CASES, LATENT_WIDTH), 1.0, 6.0, (), jnp.float32)
    basis = normal_values(key_of[6], (2, SPATIAL_POINTS, LATENT_WIDTH), LATENT_WIDTH ** -0.5, 0.3125, ((1, 512),))
    mean_fields = jnp.clip(1.5 + 1.5 * jax.random.uniform(key_of[7], (2, SPATIAL_POINTS), jnp.float32) ** level_of(key_of[7], (2, SPATIAL_POINTS), ((1, 512),), -0.2, 0.2), 1.5, 3.0)
    return {"starting_latent_vectors": starting_latent_vectors, "run_driver_case": run_driver_case, "pair_table": pair_table, "quadratic": quadratic, "linear": linear, "forcing": forcing, "basis": basis, "mean_fields": mean_fields}


time_step = 0.25
min_volume = 0.25


def reference(starting_latent_vectors, run_driver_case, pair_table, quadratic, linear, forcing, basis, mean_fields):
    run_subset = math.gcd(OUTLOOK_TRIALS, 128)
    run_subsets = OUTLOOK_TRIALS // run_subset
    first_index = pair_table[0]
    second_index = pair_table[1]
    group_numbers = jnp.arange(DRIVER_CASES, dtype=jnp.int32)
    linear_wide = linear.astype(jnp.float32)
    quadratic_wide = quadratic.astype(jnp.float32)

    def advance(packed):
        block_state, block_groups = packed
        rounded = block_state.astype(jnp.bfloat16).astype(jnp.float32)
        features = (jnp.take(block_state, first_index, axis=1) * jnp.take(block_state, second_index, axis=1)).astype(jnp.bfloat16).astype(jnp.float32)
        onehot = (block_groups[:, None] == group_numbers[None, :]).astype(jnp.float32)
        drift = jnp.dot(rounded, linear_wide, precision=lax.Precision.HIGHEST)
        drift = drift + jnp.dot(features, quadratic_wide, precision=lax.Precision.HIGHEST)
        drift = drift + jnp.dot(onehot, forcing, precision=lax.Precision.HIGHEST)
        return block_state + time_step * drift

    latent_vectors = starting_latent_vectors.reshape(run_subsets, run_subset, LATENT_WIDTH)
    groups = run_driver_case.reshape(run_subsets, run_subset)
    for step in range(STEPS):
        latent_vectors = lax.map(advance, (latent_vectors, groups))
    closing_vectors = latent_vectors.reshape(OUTLOOK_TRIALS, LATENT_WIDTH).astype(jnp.bfloat16).astype(jnp.float32)

    cell_block = math.gcd(SPATIAL_POINTS, 1024)
    cell_blocks = SPATIAL_POINTS // cell_block
    compact_coordinate_parts = jnp.transpose(basis.reshape(2, cell_blocks, cell_block, LATENT_WIDTH), (1, 0, 2, 3))
    empirical_center_each_part = jnp.transpose(mean_fields.reshape(2, cell_blocks, cell_block), (1, 0, 2))

    def lift_back_solution(packed):
        block_basis, block_mean = packed
        fields = jnp.einsum("vcr,mr->vcm", block_basis.astype(jnp.float32), closing_vectors, precision=lax.Precision.HIGHEST) + block_mean[:, :, None]
        volume = jnp.maximum(fields[0], min_volume)
        return (1.0 / volume).astype(jnp.bfloat16), (fields[1] * volume).astype(jnp.bfloat16)

    specific_weight_array, dimensionless_heat_measure = lax.map(lift_back_solution, (compact_coordinate_parts, empirical_center_each_part))
    return specific_weight_array.reshape(SPATIAL_POINTS, OUTLOOK_TRIALS), dimensionless_heat_measure.reshape(SPATIAL_POINTS, OUTLOOK_TRIALS)
```

```python
import functools

import jax
import jax.numpy as jnp
from jax import lax
from jax.experimental import pallas as pl
from jax.experimental.pallas import tpu as pltpu
from jax.sharding import PartitionSpec as P

STEPS = 2
time_step = 0.25
min_volume = 0.25
MESH = pl.DeviceIdType.MESH
TILE = 256
LINEAR_AT = 16


def wait_bytes(ref, count, sem):
    part = ref.at[pl.ds(0, count)]
    pltpu.make_async_copy(part, part, sem).wait()


def forecast_kernel(
    groups,
    feats,
    state_ref,
    cond_ref,
    pair_ref,
    quad_ref,
    linear_ref,
    forcing_ref,
    out_ref,
    first_hot,
    second_hot,
    tail_index,
    tail_rows,
    square,
    gathered,
    partials,
    arrived,
    fin,
    ag_send,
    ag_recv,
    rs_send,
    rs_recv,
    z_send,
    z_recv,
    p_send,
    p_recv,
    c_send,
    c_recv,
):
    g = lax.axis_index("grp")
    f = lax.axis_index("feat")
    core = lax.rem(f, 2)
    partner = f + 1 - 2 * core
    owned, width = state_ref.shape
    members = owned * feats
    pairs = pair_ref.shape[1]
    whole = pairs // TILE
    rest = pairs - whole * TILE
    own_inputs = linear_ref.shape[0]
    tail = tail_rows.shape[0]

    def plane_peer(r):
        return lax.rem(f + r, feats)

    barrier = pltpu.get_barrier_semaphore()

    @pl.loop(1, feats)
    def _(r):
        pl.semaphore_signal(barrier, inc=1, device_id=(g, plane_peer(r)), device_id_type=MESH)

    @pl.loop(1, groups)
    def _(d):
        pl.semaphore_signal(
            barrier, inc=1, device_id=(lax.rem(g + d, groups), f), device_id_type=MESH
        )

    state = state_ref[...]
    own_forcing = jnp.concatenate(
        [forcing_ref[pl.ds(cond_ref[k], 1), :] for k in range(owned)], axis=0
    )

    lane = lax.broadcasted_iota(jnp.int32, (1, tail), 1)
    own_input = jnp.where(
        (lane >= LINEAR_AT) & (lane < LINEAR_AT + own_inputs),
        f * own_inputs + lane - LINEAR_AT,
        -1,
    )
    tail_index[0:1, :] = own_input
    tail_index[1:2, :] = jnp.full((1, tail), -1, jnp.int32)
    tail_index[:, 0:rest] = pair_ref[:, whole * TILE : pairs]
    tail_rows[...] = jnp.zeros_like(tail_rows)
    tail_rows[0:rest, :] = quad_ref[whole * TILE : pairs, :]
    tail_rows[LINEAR_AT : LINEAR_AT + own_inputs, :] = linear_ref[...]
    tail_ones = jnp.where(own_input >= 0, 1.0, 0.0)

    for table, hot in ((0, first_hot), (1, second_hot)):
        for c in range(whole):
            number = lax.broadcasted_iota(jnp.int32, (width, TILE), 0)
            index = pair_ref[table : table + 1, c * TILE : (c + 1) * TILE]
            hot[:, c * TILE : (c + 1) * TILE] = jnp.where(number == index, 1.0, 0.0).astype(
                jnp.bfloat16
            )
        number = lax.broadcasted_iota(jnp.int32, (width, tail), 0)
        index = tail_index[table : table + 1, :]
        hot[:, whole * TILE : whole * TILE + tail] = jnp.where(number == index, 1.0, 0.0).astype(
            jnp.bfloat16
        )

    gathered[0, f] = state.astype(jnp.bfloat16)
    pl.semaphore_wait(barrier, feats - 1 + groups - 1)

    for step in range(STEPS):
        if step > 0:
            gathered[step, f] = state.astype(jnp.bfloat16)

        @pl.loop(1, feats)
        def _(r):
            pltpu.make_async_remote_copy(
                src_ref=gathered.at[step, f],
                dst_ref=gathered.at[step, f],
                send_sem=ag_send.at[step],
                recv_sem=ag_recv.at[step],
                device_id=(g, plane_peer(r)),
                device_id_type=MESH,
            ).start()

        wait_bytes(gathered.at[step], feats - 1, ag_recv.at[step])
        for r in range(feats):
            square[r * owned : (r + 1) * owned, :] = gathered[step, r].astype(jnp.float32)
        current = square[...].astype(jnp.bfloat16)

        def product(start, size, extra):
            first = jnp.dot(
                current, first_hot[:, start : start + size], preferred_element_type=jnp.float32
            )
            second = jnp.dot(
                current, second_hot[:, start : start + size], preferred_element_type=jnp.float32
            )
            if extra is not None:
                second = second + extra
            return (first * second).astype(jnp.bfloat16)

        total = jnp.dot(
            product(whole * TILE, tail, tail_ones),
            tail_rows[...],
            preferred_element_type=jnp.float32,
        )
        for c in range(whole):
            total = total + jnp.dot(
                product(c * TILE, TILE, None),
                quad_ref[c * TILE : (c + 1) * TILE, :],
                preferred_element_type=jnp.float32,
            )
        square[...] = total
        for r in range(feats):
            partials[step, r] = square[r * owned : (r + 1) * owned, :].astype(jnp.bfloat16)
        arrived[step, f] = partials[step, f]

        @pl.loop(1, feats)
        def _(r):
            peer = plane_peer(r)
            pltpu.make_async_remote_copy(
                src_ref=partials.at[step, peer],
                dst_ref=arrived.at[step, f],
                send_sem=rs_send.at[step],
                recv_sem=rs_recv.at[step],
                device_id=(g, peer),
                device_id_type=MESH,
            ).start()

        wait_bytes(arrived.at[step], feats - 1, rs_recv.at[step])
        summed = jnp.sum(arrived[step].astype(jnp.float32), axis=0)
        state = state + time_step * (summed + own_forcing)

    mine = g * feats + f
    fin[mine] = state.astype(jnp.bfloat16)

    @pl.loop(1, groups)
    def _(d):
        there = lax.rem(g + d, groups)
        pltpu.make_async_remote_copy(
            src_ref=fin.at[mine],
            dst_ref=fin.at[mine],
            send_sem=z_send,
            recv_sem=z_recv.at[g],
            device_id=(there, f),
            device_id_type=MESH,
        ).start()

    half = groups // 2
    order = [(0, (0,))] + [(d, (d, groups - d) if d != half else (d,)) for d in range(1, half + 1)]
    batches = []
    for first in range(0, len(order), 2):
        batches.append([s for _, shifts in order[first : first + 2] for s in shifts])

    def to_plane(number, batch):
        for shift in batch:
            z = lax.rem(g + shift, groups)
            chunk = z * feats + f
            if shift:
                pltpu.make_async_copy(fin.at[chunk], fin.at[chunk], z_recv.at[z]).wait()

            @pl.loop(1, feats // 2)
            def _(k):
                pltpu.make_async_remote_copy(
                    src_ref=fin.at[chunk],
                    dst_ref=fin.at[chunk],
                    send_sem=p_send,
                    recv_sem=p_recv.at[number],
                    device_id=(g, plane_peer(2 * k)),
                    device_id_type=MESH,
                ).start()

    def across(number, batch):
        wait_bytes(fin, (feats // 2 - 1) * len(batch), p_recv.at[number])
        for shift in batch:
            z = lax.rem(g + shift, groups)

            @pl.loop(0, feats // 2)
            def _(k):
                chunk = z * feats + 2 * k + core
                pltpu.make_async_remote_copy(
                    src_ref=fin.at[chunk],
                    dst_ref=fin.at[chunk],
                    send_sem=c_send,
                    recv_sem=c_recv.at[number],
                    device_id=(g, partner),
                    device_id_type=MESH,
                ).start()

    def settle(number, batch):
        wait_bytes(fin, feats // 2 * len(batch), c_recv.at[number])
        for shift in batch:
            z = lax.rem(g + shift, groups)
            for r in range(feats):
                square[r * owned : (r + 1) * owned, :] = fin[z * feats + r].astype(jnp.float32)
            out_ref[pl.ds(pl.multiple_of(z * members, members), members), :] = square[...].astype(
                jnp.bfloat16
            )

    count = len(batches)
    for number in range(count + 2):
        if number < count:
            to_plane(number, batches[number])
        if 1 <= number <= count:
            across(number - 1, batches[number - 1])
        if number >= 2:
            settle(number - 2, batches[number - 2])

    for step in range(STEPS):
        wait_bytes(gathered.at[step], feats - 1, ag_send.at[step])
        wait_bytes(partials.at[step], feats - 1, rs_send.at[step])
    wait_bytes(fin, groups - 1, z_send)
    wait_bytes(fin, (feats // 2 - 1) * groups, p_send)
    wait_bytes(fin, feats // 2 * groups, c_send)


def forecast(mesh, state, cond, pair_table, quadratic, linear, forcing):
    groups, feats = mesh.shape["grp"], mesh.shape["feat"]
    owned, width = state.shape
    pairs = pair_table.shape[1]
    whole = pairs // TILE
    tail = 128
    assert pairs - whole * TILE <= LINEAR_AT and LINEAR_AT + linear.shape[0] <= tail
    batches = (groups // 2 + 2) // 2
    vmem = pl.BlockSpec(memory_space=pltpu.VMEM)
    bf16 = jnp.bfloat16
    dma = pltpu.SemaphoreType.DMA
    return pl.pallas_call(
        functools.partial(forecast_kernel, groups, feats),
        name="forecast",
        out_shape=jax.ShapeDtypeStruct((groups * feats * owned, width), bf16),
        in_specs=[vmem, pl.BlockSpec(memory_space=pltpu.SMEM), vmem, vmem, vmem, vmem],
        out_specs=vmem,
        scratch_shapes=[
            pltpu.VMEM((width, whole * TILE + tail), bf16),
            pltpu.VMEM((width, whole * TILE + tail), bf16),
            pltpu.VMEM((2, tail), jnp.int32),
            pltpu.VMEM((tail, width), bf16),
            pltpu.VMEM((feats * owned, width), jnp.float32),
            pltpu.VMEM((STEPS, feats, owned, width), bf16),
            pltpu.VMEM((STEPS, feats, owned, width), bf16),
            pltpu.VMEM((STEPS, feats, owned, width), bf16),
            pltpu.VMEM((groups * feats, owned, width), bf16),
            dma((STEPS,)),
            dma((STEPS,)),
            dma((STEPS,)),
            dma((STEPS,)),
            dma,
            dma((groups,)),
            dma,
            dma((batches,)),
            dma,
            dma((batches,)),
        ],
        compiler_params=pltpu.CompilerParams(collective_id=0, has_side_effects=True),
    )(state, cond, pair_table, quadratic, linear, forcing)


def lift_kernel(fin_ref, basis_ref, mean_ref, weight_ref, heat_ref, means):
    cells = basis_ref.shape[1]

    @pl.when(pl.program_id(0) == 0)
    def _():
        for v in range(2):
            row = jnp.broadcast_to(mean_ref[v : v + 1, :], (128, cells))
            means[v] = row.T

    def field(v):
        product = lax.dot_general(
            basis_ref[v],
            fin_ref[...],
            (((1,), (1,)), ((), ())),
            preferred_element_type=jnp.float32,
        )
        columns = [
            product[:, at : at + 128] + means[v] for at in range(0, product.shape[1], 128)
        ]
        return jnp.concatenate(columns, axis=1)

    volume = jnp.maximum(field(0), min_volume)
    weight_ref[...] = (1.0 / volume).astype(jnp.bfloat16)
    heat_ref[...] = (field(1) * volume).astype(jnp.bfloat16)


def lift_back_solution(final, basis, mean_fields):
    members, width = final.shape
    cells = basis.shape[1]
    tile = 256
    out = jax.ShapeDtypeStruct((cells, members), jnp.bfloat16)
    block = pl.BlockSpec((cells, tile), lambda i: (0, i))
    return pl.pallas_call(
        lift_kernel,
        name="lift",
        grid=(members // tile,),
        in_specs=[
            pl.BlockSpec((tile, width), lambda i: (i, 0)),
            pl.BlockSpec((2, cells, width), lambda i: (0, 0, 0)),
            pl.BlockSpec((2, cells), lambda i: (0, 0)),
        ],
        out_specs=[block, block],
        out_shape=[out, out],
        scratch_shapes=[pltpu.VMEM((2, cells, 128), jnp.float32)],
    )(final, basis, mean_fields)


def solution(mesh):
    def per_device(state, cond, pair_table, quadratic, linear, forcing, basis, mean_fields):
        final = forecast(mesh, state, cond, pair_table, quadratic, linear, forcing)
        weight, heat = lift_back_solution(final, basis, mean_fields)
        return (weight, heat)

    return jax.shard_map(
        per_device,
        mesh=mesh,
        in_specs=(
            P(("grp", "feat"), None),
            P(("grp", "feat")),
            P(None, "feat"),
            P("feat", None),
            P("feat", None),
            P(),
            P(None, ("grp", "feat"), None),
            P(None, ("grp", "feat")),
        ),
        out_specs=(P(("grp", "feat"), None), P(("grp", "feat"), None)),
        check_vma=False,
    )
```

```python
import functools

import jax
import jax.numpy as jnp
from jax import lax
from jax.experimental import pallas as pl
from jax.experimental.pallas import tpu as pltpu
from jax.sharding import PartitionSpec as P

STEPS = 2
time_step = 0.25
min_volume = 0.25
MESH = pl.DeviceIdType.MESH
TILE = 256
LINEAR_AT = 16
SIDE = 4


def wait_bytes(ref, count, sem):
    part = ref.at[pl.ds(0, count)]
    pltpu.make_async_copy(part, part, sem).wait()


def forecast_kernel(
    groups,
    feats,
    state_hbm,
    cond_hbm,
    pair_hbm,
    quad_hbm,
    linear_hbm,
    forcing_hbm,
    out_hbm,
    state_ref,
    cond_ref,
    pair_ref,
    quad_ref,
    linear_ref,
    forcing_ref,
    first_hot,
    second_hot,
    tail_index,
    tail_rows,
    gathered,
    partials,
    arrived,
    fin,
    rows,
    load_sem,
    ag_send,
    ag_recv,
    rs_send,
    rs_recv,
    z_send,
    z_recv,
    plane_send,
    plane_recv,
    cross_send,
    cross_recv,
    store_sem,
):
    g = lax.axis_index("grp")
    f = lax.axis_index("feat")
    core = lax.rem(f, 2)
    at_x = lax.rem(f // 2, SIDE)
    at_y = f // (2 * SIDE)
    owned, width = state_ref.shape
    members = owned * feats
    pairs = pair_ref.shape[1]
    whole = pairs // TILE
    rest = pairs - whole * TILE
    own_inputs = linear_ref.shape[0]
    tail = tail_rows.shape[0]
    half = groups // 2

    def plane_peer(r):
        return lax.rem(f + r, feats)

    barrier = pltpu.get_barrier_semaphore()

    @pl.loop(1, groups)
    def _(d):
        pl.semaphore_signal(
            barrier, inc=1, device_id=(lax.rem(g + d, groups), f), device_id_type=MESH
        )

    @pl.loop(1, feats)
    def _(r):
        pl.semaphore_signal(barrier, inc=1, device_id=(g, plane_peer(r)), device_id_type=MESH)

    loads = [
        pltpu.make_async_copy(source, target, load_sem.at[k])
        for k, (source, target) in enumerate(
            (
                (state_hbm, state_ref),
                (cond_hbm, cond_ref),
                (forcing_hbm, forcing_ref),
                (pair_hbm, pair_ref),
                (linear_hbm, linear_ref),
                (quad_hbm, quad_ref),
            )
        )
    ]
    for load in loads:
        load.start()
    for load in loads[:3]:
        load.wait()
    state = state_ref[...]
    own_forcing = jnp.concatenate(
        [forcing_ref[pl.ds(cond_ref[k], 1), :] for k in range(owned)], axis=0
    )
    gathered[0, f] = state.astype(jnp.bfloat16)
    pl.semaphore_wait(barrier, feats - 1 + groups - 1)

    def gather_states(step):
        @pl.loop(1, feats)
        def _(r):
            pltpu.make_async_remote_copy(
                src_ref=gathered.at[step, f],
                dst_ref=gathered.at[step, f],
                send_sem=ag_send.at[step],
                recv_sem=ag_recv.at[step],
                device_id=(g, plane_peer(r)),
                device_id_type=MESH,
            ).start()

    gather_states(0)
    for load in loads[3:]:
        load.wait()
    lane = lax.broadcasted_iota(jnp.int32, (1, tail), 1)
    own_input = jnp.where(
        (lane >= LINEAR_AT) & (lane < LINEAR_AT + own_inputs),
        f * own_inputs + lane - LINEAR_AT,
        -1,
    )
    tail_index[0:1, :] = own_input
    tail_index[1:2, :] = jnp.full((1, tail), -1, jnp.int32)
    tail_index[:, 0:rest] = pair_ref[:, whole * TILE : pairs]
    tail_rows[...] = jnp.zeros_like(tail_rows)
    tail_rows[0:rest, :] = quad_ref[whole * TILE : pairs, :]
    tail_rows[LINEAR_AT : LINEAR_AT + own_inputs, :] = linear_ref[...]
    tail_ones = jnp.where(own_input >= 0, 1.0, 0.0)

    for table, hot in ((0, first_hot), (1, second_hot)):
        for c in range(whole):
            number = lax.broadcasted_iota(jnp.int32, (width, TILE), 0)
            index = pair_ref[table : table + 1, c * TILE : (c + 1) * TILE]
            hot[:, c * TILE : (c + 1) * TILE] = jnp.where(number == index, 1.0, 0.0).astype(
                jnp.bfloat16
            )
        number = lax.broadcasted_iota(jnp.int32, (width, tail), 0)
        index = tail_index[table : table + 1, :]
        hot[:, whole * TILE : whole * TILE + tail] = jnp.where(number == index, 1.0, 0.0).astype(
            jnp.bfloat16
        )

    for step in range(STEPS):
        if step > 0:
            gathered[step, f] = state.astype(jnp.bfloat16)
            gather_states(step)

        wait_bytes(gathered.at[step], feats - 1, ag_recv.at[step])
        current = gathered[step].reshape(members, width)

        def product(start, size, extra):
            first = jnp.dot(
                current, first_hot[:, start : start + size], preferred_element_type=jnp.float32
            )
            second = jnp.dot(
                current, second_hot[:, start : start + size], preferred_element_type=jnp.float32
            )
            if extra is not None:
                second = second + extra
            return (first * second).astype(jnp.bfloat16)

        total = jnp.dot(
            product(whole * TILE, tail, tail_ones),
            tail_rows[...],
            preferred_element_type=jnp.float32,
        )
        for c in range(whole):
            total = total + jnp.dot(
                product(c * TILE, TILE, None),
                quad_ref[c * TILE : (c + 1) * TILE, :],
                preferred_element_type=jnp.float32,
            )
        partials[step] = total.astype(jnp.bfloat16).reshape(feats, owned, width)
        arrived[step, f] = partials[step, f]

        @pl.loop(1, feats)
        def _(r):
            peer = plane_peer(r)
            pltpu.make_async_remote_copy(
                src_ref=partials.at[step, peer],
                dst_ref=arrived.at[step, f],
                send_sem=rs_send.at[step],
                recv_sem=rs_recv.at[step],
                device_id=(g, peer),
                device_id_type=MESH,
            ).start()

        wait_bytes(arrived.at[step], feats - 1, rs_recv.at[step])
        summed = jnp.sum(arrived[step].astype(jnp.float32), axis=0)
        state = state + time_step * (summed + own_forcing)

    fin[half, at_y, at_x, core] = state.astype(jnp.bfloat16)

    @pl.loop(1, groups)
    def _(k):
        d = lax.rem(half + groups + (1 - 2 * lax.rem(k, 2)) * (k // 2), groups)
        position = lax.rem(groups + half - d, groups)
        pltpu.make_async_remote_copy(
            src_ref=fin.at[half, at_y, at_x, core],
            dst_ref=fin.at[position, at_y, at_x, core],
            send_sem=z_send,
            recv_sem=z_recv.at[position],
            device_id=(lax.rem(g + d, groups), f),
            device_id_type=MESH,
        ).start()

    plane_copies = {}
    cross_copies = {}
    stores = []

    def to_plane(number, path, stage):
        start, size = batches[number][path]
        span = pl.ds(start, size)
        along_x = stage == path
        if stage == 0:
            view = fin.at[span, at_y, at_x, core]
        elif along_x:
            view = fin.at[span, :, at_x, core]
        else:
            view = fin.at[span, at_y, :, core]
        for k, by in enumerate((2, 1, 3)):
            y, x = at_y, at_x
            if along_x:
                x = lax.rem(at_x + by, SIDE)
            else:
                y = lax.rem(at_y + by, SIDE)
            copy = pltpu.make_async_remote_copy(
                src_ref=view,
                dst_ref=view,
                send_sem=plane_send.at[number, path, stage, k],
                recv_sem=plane_recv.at[number, path, stage, k],
                device_id=(g, (y * SIDE + x) * 2 + core),
                device_id_type=MESH,
            )
            plane_copies[number, path, stage, k] = copy
            copy.start()

    def first_stage(number):
        for path in range(2):
            start, size = batches[number][path]
            for position in range(start, start + size):
                if position != half:
                    spot = fin.at[position, at_y, at_x, core]
                    pltpu.make_async_copy(spot, spot, z_recv.at[position]).wait()
            to_plane(number, path, 0)

    def second_stage(number):
        for path in range(2):
            for k in range(3):
                plane_copies[number, path, 0, k].wait_recv()
            to_plane(number, path, 1)

    def across(number):
        for path in range(2):
            for k in range(3):
                plane_copies[number, path, 1, k].wait_recv()
            start, size = batches[number][path]
            view = fin.at[pl.ds(start, size), :, :, core]
            copy = pltpu.make_async_remote_copy(
                src_ref=view,
                dst_ref=view,
                send_sem=cross_send.at[number, path],
                recv_sem=cross_recv.at[number, path],
                device_id=(g, f + 1 - 2 * core),
                device_id_type=MESH,
            )
            cross_copies[number, path] = copy
            copy.start()

    def settle(number):
        for path in range(2):
            cross_copies[number, path].wait_recv()
            start, size = batches[number][path]
            for position in range(start, start + size):
                z = lax.rem(g + position + half, groups)
                rows[position] = fin[position].reshape(members, width)
                store = pltpu.make_async_copy(
                    rows.at[position],
                    out_hbm.at[pl.ds(pl.multiple_of(z * members, members), members)],
                    store_sem.at[position],
                )
                store.start()
                stores.append(store)

    quarter = half // 2
    batches = (
        ((half, quarter), (half - quarter, quarter)),
        ((half + quarter, half - quarter), (0, half - quarter)),
    )
    first_stage(0)
    second_stage(0)
    first_stage(1)
    second_stage(1)
    across(0)
    settle(0)
    across(1)
    settle(1)

    for step in range(STEPS):
        wait_bytes(gathered.at[step], feats - 1, ag_send.at[step])
        wait_bytes(partials.at[step], feats - 1, rs_send.at[step])
    sent = fin.at[pl.ds(0, groups - 1), 0, 0, 0]
    pltpu.make_async_copy(sent, sent, z_send).wait()
    for copy in (*plane_copies.values(), *cross_copies.values()):
        copy.wait_send()
    for store in stores:
        store.wait()


def forecast(mesh, state, cond, pair_table, quadratic, linear, forcing):
    groups, feats = mesh.shape["grp"], mesh.shape["feat"]
    owned, width = state.shape
    pairs = pair_table.shape[1]
    whole = pairs // TILE
    tail = 128
    assert pairs - whole * TILE <= LINEAR_AT and LINEAR_AT + linear.shape[0] <= tail
    assert feats == 2 * SIDE * SIDE and groups % 4 == 0
    anywhere = pl.BlockSpec(memory_space=pl.ANY)
    bf16 = jnp.bfloat16
    dma = pltpu.SemaphoreType.DMA
    return pl.pallas_call(
        functools.partial(forecast_kernel, groups, feats),
        name="forecast",
        out_shape=jax.ShapeDtypeStruct((groups * feats * owned, width), bf16),
        in_specs=[anywhere] * 6,
        out_specs=anywhere,
        scratch_shapes=[
            pltpu.VMEM(state.shape, state.dtype),
            pltpu.SMEM(cond.shape, cond.dtype),
            pltpu.VMEM(pair_table.shape, pair_table.dtype),
            pltpu.VMEM(quadratic.shape, quadratic.dtype),
            pltpu.VMEM(linear.shape, linear.dtype),
            pltpu.VMEM(forcing.shape, forcing.dtype),
            pltpu.VMEM((width, whole * TILE + tail), bf16),
            pltpu.VMEM((width, whole * TILE + tail), bf16),
            pltpu.VMEM((2, tail), jnp.int32),
            pltpu.VMEM((tail, width), bf16),
            pltpu.VMEM((STEPS, feats, owned, width), bf16),
            pltpu.VMEM((STEPS, feats, owned, width), bf16),
            pltpu.VMEM((STEPS, feats, owned, width), bf16),
            pltpu.VMEM((groups, SIDE, SIDE, 2, owned, width), bf16),
            pltpu.VMEM((groups, feats * owned, width), bf16),
            dma((6,)),
            dma((STEPS,)),
            dma((STEPS,)),
            dma((STEPS,)),
            dma((STEPS,)),
            dma,
            dma((groups,)),
            dma((2, 2, 2, 3)),
            dma((2, 2, 2, 3)),
            dma((2, 2)),
            dma((2, 2)),
            dma((groups,)),
        ],
        compiler_params=pltpu.CompilerParams(collective_id=0, has_side_effects=True),
    )(state, cond, pair_table, quadratic, linear, forcing)


def lift_kernel(fin_ref, basis_ref, mean_ref, weight_ref, heat_ref, means):
    cells = basis_ref.shape[1]

    @pl.when(pl.program_id(0) == 0)
    def _():
        for v in range(2):
            row = jnp.broadcast_to(mean_ref[v : v + 1, :], (128, cells))
            means[v] = row.T

    def field(v):
        product = lax.dot_general(
            basis_ref[v],
            fin_ref[...],
            (((1,), (1,)), ((), ())),
            preferred_element_type=jnp.float32,
        )
        columns = [
            product[:, at : at + 128] + means[v] for at in range(0, product.shape[1], 128)
        ]
        return jnp.concatenate(columns, axis=1)

    volume = jnp.maximum(field(0), min_volume)
    weight_ref[...] = (1.0 / volume).astype(jnp.bfloat16)
    heat_ref[...] = (field(1) * volume).astype(jnp.bfloat16)


def lift_back_solution(final, basis, mean_fields):
    members, width = final.shape
    cells = basis.shape[1]
    tile = 1024
    out = jax.ShapeDtypeStruct((cells, members), jnp.bfloat16)
    block = pl.BlockSpec((cells, tile), lambda i: (0, i))
    return pl.pallas_call(
        lift_kernel,
        name="lift",
        grid=(members // tile,),
        in_specs=[
            pl.BlockSpec((tile, width), lambda i: (i, 0)),
            pl.BlockSpec((2, cells, width), lambda i: (0, 0, 0)),
            pl.BlockSpec((2, cells), lambda i: (0, 0)),
        ],
        out_specs=[block, block],
        out_shape=[out, out],
        scratch_shapes=[pltpu.VMEM((2, cells, 128), jnp.float32)],
    )(final, basis, mean_fields)


def solution(mesh):
    def per_device(state, cond, pair_table, quadratic, linear, forcing, basis, mean_fields):
        final = forecast(mesh, state, cond, pair_table, quadratic, linear, forcing)
        weight, heat = lift_back_solution(final, basis, mean_fields)
        return (weight, heat)

    return jax.shard_map(
        per_device,
        mesh=mesh,
        in_specs=(
            P(("grp", "feat"), None),
            P(("grp", "feat")),
            P(None, "feat"),
            P("feat", None),
            P("feat", None),
            P(),
            P(None, ("grp", "feat"), None),
            P(None, ("grp", "feat")),
        ),
        out_specs=(P(("grp", "feat"), None), P(("grp", "feat"), None)),
        check_vma=False,
    )
```

```python
import functools

import jax
import jax.numpy as jnp
from jax import lax
from jax.experimental import pallas as pl
from jax.experimental.pallas import tpu as pltpu
from jax.sharding import PartitionSpec as P

STEPS = 2
time_step = 0.25
min_volume = 0.25
MESH = pl.DeviceIdType.MESH
TILE = 256
LINEAR_AT = 16
SIDE = 4
SPANS = ((4, 8), (12, 4), (0, 4))


def wait_bytes(ref, count, sem):
    part = ref.at[pl.ds(0, count)]
    pltpu.make_async_copy(part, part, sem).wait()


def forecast_kernel(
    groups,
    feats,
    state_hbm,
    cond_hbm,
    pair_hbm,
    quad_hbm,
    linear_hbm,
    forcing_hbm,
    basis_hbm,
    mean_hbm,
    weight_ref,
    heat_ref,
    state_ref,
    cond_ref,
    pair_ref,
    quad_ref,
    linear_ref,
    forcing_ref,
    first_hot,
    second_hot,
    tail_index,
    tail_rows,
    gathered,
    partials,
    arrived,
    fin,
    basis_ref,
    mean_ref,
    means,
    load_sem,
    ag_send,
    ag_recv,
    rs_send,
    rs_recv,
    z_send,
    z_recv,
    plane_send,
    plane_recv,
    cross_send,
    cross_recv,
):
    g = lax.axis_index("grp")
    f = lax.axis_index("feat")
    core = lax.rem(f, 2)
    at_x = lax.rem(f // 2, SIDE)
    at_y = f // (2 * SIDE)
    owned, width = state_ref.shape
    members = owned * feats
    pairs = pair_ref.shape[1]
    whole = pairs // TILE
    rest = pairs - whole * TILE
    own_inputs = linear_ref.shape[0]
    tail = tail_rows.shape[0]
    half = groups // 2

    def plane_peer(r):
        return lax.rem(f + r, feats)

    def far_peers(cores=True):
        shifts = [
            (y, x, c) for y in range(SIDE) for x in range(SIDE) for c in range(1 + cores)
        ]
        shifts.sort(key=lambda s: -(min(s[0], SIDE - s[0]) + min(s[1], SIDE - s[1])))
        for y, x, c in (t for t in shifts if any(t)):
            to_y, to_x = lax.rem(at_y + y, SIDE), lax.rem(at_x + x, SIDE)
            yield (to_y * SIDE + to_x) * 2 + (1 - core if c else core)

    barrier = pltpu.get_barrier_semaphore()

    @pl.loop(1, groups)
    def _(d):
        pl.semaphore_signal(
            barrier, inc=1, device_id=(lax.rem(g + d, groups), f), device_id_type=MESH
        )

    @pl.loop(1, feats)
    def _(r):
        pl.semaphore_signal(barrier, inc=1, device_id=(g, plane_peer(r)), device_id_type=MESH)

    loads = [
        pltpu.make_async_copy(source, target, load_sem.at[k])
        for k, (source, target) in enumerate(
            (
                (state_hbm, state_ref),
                (cond_hbm, cond_ref),
                (forcing_hbm, forcing_ref),
                (pair_hbm, pair_ref),
                (linear_hbm, linear_ref),
                (quad_hbm, quad_ref),
                (basis_hbm, basis_ref),
                (mean_hbm, mean_ref),
            )
        )
    ]
    for load in loads:
        load.start()
    for load in loads[:3]:
        load.wait()
    state = state_ref[...]
    own_forcing = jnp.concatenate(
        [forcing_ref[pl.ds(cond_ref[k], 1), :] for k in range(owned)], axis=0
    )
    gathered[0, f] = state.astype(jnp.bfloat16)
    pl.semaphore_wait(barrier, feats - 1 + groups - 1)

    def gather_states(step):
        for peer in far_peers():
            pltpu.make_async_remote_copy(
                src_ref=gathered.at[step, f],
                dst_ref=gathered.at[step, f],
                send_sem=ag_send.at[step],
                recv_sem=ag_recv.at[step],
                device_id=(g, peer),
                device_id_type=MESH,
            ).start()

    gather_states(0)
    for load in loads[3:6]:
        load.wait()
    lane = lax.broadcasted_iota(jnp.int32, (1, tail), 1)
    own_input = jnp.where(
        (lane >= LINEAR_AT) & (lane < LINEAR_AT + own_inputs),
        f * own_inputs + lane - LINEAR_AT,
        -1,
    )
    tail_index[0:1, :] = own_input
    tail_index[1:2, :] = jnp.full((1, tail), -1, jnp.int32)
    tail_index[:, 0:rest] = pair_ref[:, whole * TILE : pairs]
    tail_rows[...] = jnp.zeros_like(tail_rows)
    tail_rows[0:rest, :] = quad_ref[whole * TILE : pairs, :]
    tail_rows[LINEAR_AT : LINEAR_AT + own_inputs, :] = linear_ref[...]
    tail_ones = jnp.where(own_input >= 0, 1.0, 0.0)

    for table, hot in ((0, first_hot), (1, second_hot)):
        for c in range(whole):
            number = lax.broadcasted_iota(jnp.int32, (width, TILE), 0)
            index = pair_ref[table : table + 1, c * TILE : (c + 1) * TILE]
            hot[:, c * TILE : (c + 1) * TILE] = jnp.where(number == index, 1.0, 0.0).astype(
                jnp.bfloat16
            )
        number = lax.broadcasted_iota(jnp.int32, (width, tail), 0)
        index = tail_index[table : table + 1, :]
        hot[:, whole * TILE : whole * TILE + tail] = jnp.where(number == index, 1.0, 0.0).astype(
            jnp.bfloat16
        )

    for step in range(STEPS):
        if step > 0:
            gathered[step, f] = state.astype(jnp.bfloat16)
            gather_states(step)

        wait_bytes(gathered.at[step], feats - 1, ag_recv.at[step])
        current = gathered[step].reshape(members, width)

        def product(start, size, extra):
            first = jnp.dot(
                current, first_hot[:, start : start + size], preferred_element_type=jnp.float32
            )
            second = jnp.dot(
                current, second_hot[:, start : start + size], preferred_element_type=jnp.float32
            )
            if extra is not None:
                second = second + extra
            return (first * second).astype(jnp.bfloat16)

        total = jnp.dot(
            product(whole * TILE, tail, tail_ones),
            tail_rows[...],
            preferred_element_type=jnp.float32,
        )
        for c in range(whole):
            total = total + jnp.dot(
                product(c * TILE, TILE, None),
                quad_ref[c * TILE : (c + 1) * TILE, :],
                preferred_element_type=jnp.float32,
            )
        partials[step] = total.astype(jnp.bfloat16).reshape(feats, owned, width)
        arrived[step, f] = partials[step, f]

        for peer in far_peers():
            pltpu.make_async_remote_copy(
                src_ref=partials.at[step, peer],
                dst_ref=arrived.at[step, f],
                send_sem=rs_send.at[step],
                recv_sem=rs_recv.at[step],
                device_id=(g, peer),
                device_id_type=MESH,
            ).start()

        wait_bytes(arrived.at[step], feats - 1, rs_recv.at[step])
        summed = jnp.sum(arrived[step].astype(jnp.float32), axis=0)
        state = state + time_step * (summed + own_forcing)

    fin[half, at_y, at_x, core] = state.astype(jnp.bfloat16)

    @pl.loop(1, groups)
    def _(k):
        d = lax.rem(groups + (2 * lax.rem(k, 2) - 1) * ((k + 1) // 2), groups)
        position = lax.rem(groups + half - d, groups)
        pltpu.make_async_remote_copy(
            src_ref=fin.at[half, at_y, at_x, core],
            dst_ref=fin.at[position, at_y, at_x, core],
            send_sem=z_send,
            recv_sem=z_recv.at[position],
            device_id=(lax.rem(g + d, groups), f),
            device_id_type=MESH,
        ).start()

    for load in loads[6:]:
        load.wait()
    for v in range(2):
        means[v] = jnp.broadcast_to(mean_ref[v : v + 1, :], (128, mean_ref.shape[1])).T
    sends = []
    cross_copies = {}

    def to_plane(number):
        start, size = spans[number]
        for position in range(start, start + size):
            if position != half:
                spot = fin.at[position, at_y, at_x, core]
                pltpu.make_async_copy(spot, spot, z_recv.at[position]).wait()
        view = fin.at[pl.ds(start, size), at_y, at_x, core]
        for k, peer in enumerate(far_peers(False)):
            copy = pltpu.make_async_remote_copy(
                src_ref=view,
                dst_ref=view,
                send_sem=plane_send.at[number, k],
                recv_sem=plane_recv.at[number],
                device_id=(g, peer),
                device_id_type=MESH,
            )
            copy.start()
            sends.append(copy)

    def across(number):
        start, size = spans[number]
        span = pl.ds(start, size)
        landed = fin.at[pl.ds(0, SIDE * SIDE - 1), :, pl.ds(0, size // SIDE), core]
        pltpu.make_async_copy(landed, landed, plane_recv.at[number]).wait()
        view = fin.at[span, :, :, core]
        copy = pltpu.make_async_remote_copy(
            src_ref=view,
            dst_ref=view,
            send_sem=cross_send.at[number],
            recv_sem=cross_recv.at[number],
            device_id=(g, f + 1 - 2 * core),
            device_id_type=MESH,
        )
        cross_copies[number] = copy
        copy.start()

    def settle(number):
        cross_copies[number].wait_recv()
        start, size = spans[number]
        for position in range(start, start + size, 2):
            final = fin[position : position + 2].reshape(2 * members, width)
            spots = [
                pl.ds(pl.multiple_of(lax.rem(g + p + half, groups) * members, members), members)
                for p in (position, position + 1)
            ]

            def field(v):
                product = lax.dot_general(
                    basis_ref[v], final, (((1,), (1,)), ((), ())), preferred_element_type=jnp.float32
                )
                return [product[:, at : at + members] + means[v] for at in (0, members)]

            for spot, volume, pressure in zip(spots, field(0), field(1)):
                volume = jnp.maximum(volume, min_volume)
                weight_ref[:, spot] = (1.0 / volume).astype(jnp.bfloat16)
                heat_ref[:, spot] = (pressure * volume).astype(jnp.bfloat16)

    spans = SPANS
    for number in range(len(spans)):
        to_plane(number)
    for number in range(len(spans) + 1):
        if number < len(spans):
            across(number)
        if number > 0:
            settle(number - 1)

    for step in range(STEPS):
        wait_bytes(gathered.at[step], feats - 1, ag_send.at[step])
        wait_bytes(partials.at[step], feats - 1, rs_send.at[step])
    sent = fin.at[pl.ds(0, groups - 1), 0, 0, 0]
    pltpu.make_async_copy(sent, sent, z_send).wait()
    for copy in (*sends, *cross_copies.values()):
        copy.wait_send()


def forecast(mesh, state, cond, pair_table, quadratic, linear, forcing, basis, mean_fields):
    groups, feats = mesh.shape["grp"], mesh.shape["feat"]
    owned, width = state.shape
    pairs = pair_table.shape[1]
    whole = pairs // TILE
    tail = 128
    cells = basis.shape[1]
    assert feats * owned == 128
    assert pairs - whole * TILE <= LINEAR_AT and LINEAR_AT + linear.shape[0] <= tail
    assert feats == 2 * SIDE * SIDE and groups == 16
    anywhere = pl.BlockSpec(memory_space=pl.ANY)
    bf16 = jnp.bfloat16
    dma = pltpu.SemaphoreType.DMA
    return pl.pallas_call(
        functools.partial(forecast_kernel, groups, feats),
        name="forecast",
        out_shape=[pltpu.VMEM((cells, groups * feats * owned), bf16)] * 2,
        in_specs=[anywhere] * 8,
        out_specs=[pl.BlockSpec(memory_space=pltpu.VMEM)] * 2,
        scratch_shapes=[
            pltpu.VMEM(state.shape, state.dtype),
            pltpu.SMEM(cond.shape, cond.dtype),
            pltpu.VMEM(pair_table.shape, pair_table.dtype),
            pltpu.VMEM(quadratic.shape, quadratic.dtype),
            pltpu.VMEM(linear.shape, linear.dtype),
            pltpu.VMEM(forcing.shape, forcing.dtype),
            pltpu.VMEM((width, whole * TILE + tail), bf16),
            pltpu.VMEM((width, whole * TILE + tail), bf16),
            pltpu.VMEM((2, tail), jnp.int32),
            pltpu.VMEM((tail, width), bf16),
            pltpu.VMEM((STEPS, feats, owned, width), bf16),
            pltpu.VMEM((STEPS, feats, owned, width), bf16),
            pltpu.VMEM((STEPS, feats, owned, width), bf16),
            pltpu.VMEM((groups, SIDE, SIDE, 2, owned, width), bf16),
            pltpu.VMEM(basis.shape, bf16),
            pltpu.VMEM(mean_fields.shape, jnp.float32),
            pltpu.VMEM((2, cells, 128), jnp.float32),
            dma((8,)),
            dma((STEPS,)),
            dma((STEPS,)),
            dma((STEPS,)),
            dma((STEPS,)),
            dma,
            dma((groups,)),
            dma((len(SPANS), SIDE * SIDE - 1)),
            dma((len(SPANS),)),
            dma((len(SPANS),)),
            dma((len(SPANS),)),
        ],
        compiler_params=pltpu.CompilerParams(collective_id=0, has_side_effects=True),
    )(state, cond, pair_table, quadratic, linear, forcing, basis, mean_fields)


def solution(mesh):
    def per_device(state, cond, pair_table, quadratic, linear, forcing, basis, mean_fields):
        weight, heat = forecast(
            mesh, state, cond, pair_table, quadratic, linear, forcing, basis, mean_fields
        )
        return (weight, heat)

    return jax.shard_map(
        per_device,
        mesh=mesh,
        in_specs=(
            P(("grp", "feat"), None),
            P(("grp", "feat")),
            P(None, "feat"),
            P("feat", None),
            P("feat", None),
            P(),
            P(None, ("grp", "feat"), None),
            P(None, ("grp", "feat")),
        ),
        out_specs=(P(("grp", "feat"), None), P(("grp", "feat"), None)),
        check_vma=False,
    )
```
